32 devices in a mesh: rep: 16 (over z, y, x), grp: 2 (over core).
Axes of the slice: x: 2, y: 2, z: 4, core: 2. Of those that a mesh axis runs over, the one named last changes fastest.
Arguments:
- inputs: float32 [16, 1024, 768], P('rep', 'grp'), may hold values from -6 to 6
- clip_lengths: int32 [16], P('rep'), may hold values from 960 to 1024, as said below
- first_gain: bfloat16 [768], P('grp'), may hold values from 0.5 to 1.5
- first_shift: bfloat16 [768], P('grp'), may hold values from -4 to 4
- query_weight: bfloat16 [768, 768], P('grp'), may hold values from -0.21875 to 0.21875
- query_bias: bfloat16 [768], P('grp'), may hold values from -6 to 6
- key_weight: bfloat16 [768, 768], P('grp'), may hold values from -0.21875 to 0.21875
- value_weight: bfloat16 [768, 768], P('grp'), may hold values from -0.21875 to 0.21875
- value_bias: bfloat16 [768], P('grp'), may hold values from -0.75 to 0.75
- output_weight: bfloat16 [768, 768], P('grp'), may hold values from -8 to 8
- output_bias: bfloat16 [768], P('grp'), may hold values from -2 to 2
- second_gain: bfloat16 [768], P('grp'), may hold values from 0.5 to 1.5
- second_shift: bfloat16 [768], P('grp'), may hold values from -4 to 4
- up_weight: bfloat16 [768, 3072], P('grp'), may hold values from -0.21875 to 0.21875
- up_bias: bfloat16 [3072], P('grp'), may hold values from -6 to 6
- down_weight: bfloat16 [3072, 768], P('grp'), may hold values from -0.109375 to 0.109375
- down_bias: bfloat16 [768], P('grp'), may hold values from -2 to 2
- out_grad: float32 [16, 1024, 768], P('rep', 'grp'), may hold values from -6 to 6
Outputs:
- block_out: float32 [16, 1024, 768], P('rep', 'grp')
- input_grad: float32 [16, 1024, 768], P('rep', 'grp')
- first_gain_grad: float32 [768], P('grp')
- first_shift_grad: float32 [768], P('grp')
- query_weight_grad: float32 [768, 768], P('grp')
- query_bias_grad: float32 [768], P('grp')
- key_weight_grad: float32 [768, 768], P('grp')
- value_weight_grad: float32 [768, 768], P('grp')
- value_bias_grad: float32 [768], P('grp')
- output_weight_grad: float32 [768, 768], P('grp')
- output_bias_grad: float32 [768], P('grp')
- second_gain_grad: float32 [768], P('grp')
- second_shift_grad: float32 [768], P('grp')
- up_weight_grad: float32 [768, 3072], P('grp')
- up_bias_grad: float32 [3072], P('grp')
- down_weight_grad: float32 [3072, 768], P('grp')
- down_bias_grad: float32 [768], P('grp')
The draws below stay inside these ranges and needn't reach their ends.
Inputs may be any that keep to these rules, and one draw needn't show every extreme that they name: `clip_lengths`: every clip has at least 960 valid frames; some clip is fully valid.
All inputs are finite; a program needn't handle non-finite values.
Results may differ from the reference program's by a relative error of at most 0.018.
Values may be sent and summed in bfloat16 or wider, within the bound.
A program may use at most 192 MiB of HBM per device.

```python
import jax
import jax.numpy as jnp
from jax import lax

D = 768
HEADS = 12
HEAD_DIM = 64
FF = 3072
FRAMES = 1024
CLIPS = 16


def draw_clip_lengths(key, part):
    lengths = jax.random.randint(key, (CLIPS,), FRAMES - FRAMES // 16, FRAMES + 1)
    return lengths.at[0].set(FRAMES).astype(jnp.int32)


def levels(stream_key, dims, shards, least, high):
    factor_of, own = 1.0, jax.random.fold_in(stream_key, 6)
    for axis_at, blocks in shards:
        draws = jnp.exp(jax.random.uniform(jax.random.fold_in(own, axis_at), (blocks,), jnp.float32, least / len(shards), high / len(shards)))
        factor_of = factor_of * jnp.repeat(draws, dims[axis_at] // blocks).reshape([-1 if axis == axis_at else 1 for axis in range(len(dims))])
    return factor_of


def noise(rng, dims, scale, limit, shards=(), kind=jnp.bfloat16):
    loudness = levels(rng, dims, shards, -0.22, 0.18) if shards else 1.0
    entries = jax.random.normal(rng, dims, jnp.float32) * scale * loudness
    return jnp.minimum(jnp.maximum(entries, -limit), limit).astype(kind)


def setup_inputs(seed: int = 0) -> dict:
    key_of = jax.random.split(jax.random.key(seed), 19)
    return {
        "inputs": noise(key_of[0], (CLIPS, FRAMES, D), 1.0, 6.0, ((0, 16), (1, 2)), jnp.float32),
        "clip_lengths": draw_clip_lengths(jax.random.fold_in(key_of[18], 71), 0),
        "first_gain": jnp.clip(1.0 + 0.1 * jax.random.normal(key_of[2], (D,), jnp.float32), 0.5, 1.5).astype(jnp.bfloat16),
        "first_shift": noise(key_of[3], (D,), 0.3, 4.0, ((0, 2),)),
        "query_weight": noise(key_of[4], (D, D), D ** -0.5, 0.21875, ((0, 2),)),
        "query_bias": noise(key_of[5], (D,), 0.5, 6.0, ((0, 2),)),
        "key_weight": noise(key_of[6], (D, D), D ** -0.5, 0.21875, ((0, 2),)),
        "value_weight": noise(key_of[7], (D, D), D ** -0.5, 0.21875, ((0, 2),)),
        "value_bias": noise(key_of[8], (D,), 0.05, 0.75, ((0, 2),)),
        "output_weight": noise(key_of[9], (D, D), 1.0, 8.0, ((0, 2),)),
        "output_bias": jnp.clip(jax.random.uniform(key_of[10], (D,), jnp.float32, -2.0, 2.0) * levels(key_of[10], (D,), ((0, 2),), -0.4, 0.0), -2.0, 2.0).astype(jnp.bfloat16),
        "second_gain": jnp.clip(1.0 + 0.1 * jax.random.normal(key_of[11], (D,), jnp.float32), 0.5, 1.5).astype(jnp.bfloat16),
        "second_shift": noise(key_of[12], (D,), 0.3, 4.0, ((0, 2),)),
        "up_weight": noise(key_of[13], (D, FF), D ** -0.5, 0.21875, ((0, 2),)),
        "up_bias": noise(key_of[14], (FF,), 0.5, 6.0, ((0, 2),)),
        "down_weight": noise(key_of[15], (FF, D), FF ** -0.5, 0.109375, ((0, 2),)),
        "down_bias": jnp.clip(jax.random.uniform(key_of[16], (D,), jnp.float32, -2.0, 2.0) * levels(key_of[16], (D,), ((0, 2),), -0.4, 0.0), -2.0, 2.0).astype(jnp.bfloat16),
        "out_grad": noise(key_of[17], (CLIPS, FRAMES, D), 1.0, 6.0, ((0, 16), (1, 2)), jnp.float32),
    }


EPS = 1e-05
NEG = -1e+30
SQRT_HALF = 0.7071067811865476
INV_ROOT_TWO_PI = 0.3989422804014327

def layer_norm(rows, gain, shift):
    average = lax.optimization_barrier(jnp.mean(rows, axis=-1, keepdims=True))
    centered = rows - average
    inverse = lax.rsqrt(lax.optimization_barrier(jnp.mean(centered * centered, axis=-1, keepdims=True)) + EPS)
    normed = centered * inverse
    result = normed * gain.astype(jnp.float32) + shift.astype(jnp.float32)
    return (result.astype(jnp.bfloat16), normed, inverse)

def norm_backward(upstream, normed, inverse, gain):
    scaled = upstream * gain.astype(jnp.float32)
    result = inverse * (scaled - lax.optimization_barrier(jnp.mean(scaled, axis=-1, keepdims=True)) - normed * lax.optimization_barrier(jnp.mean(scaled * normed, axis=-1, keepdims=True)))
    rows_axes = tuple(range(upstream.ndim - 1))
    return (result, lax.optimization_barrier(jnp.sum(upstream * normed, axis=rows_axes)), lax.optimization_barrier(jnp.sum(upstream, axis=rows_axes)))

def gelu_value(pre):
    return 0.5 * pre * (1.0 + lax.erf(pre * SQRT_HALF))

def gelu_slope(pre):
    return 0.5 * (1.0 + lax.erf(pre * SQRT_HALF)) + pre * jnp.exp(-0.5 * pre * pre) * INV_ROOT_TWO_PI

def matmul(left, right):
    return jnp.dot(left, right, preferred_element_type=jnp.float32)

def back_matmul(left, right):
    return jnp.dot(left, right.T, preferred_element_type=jnp.float32)

def outer_sum(left, right):
    return jnp.dot(left.T, right, preferred_element_type=jnp.float32)

def clip_pass(params, rows, upstream, length):
    gain_before, shift_before, query_matrix, query_offset, key_matrix, value_matrix, value_offset, output_matrix, output_offset, gain_middle, shift_middle, up_matrix, up_offset, down_matrix, down_offset = params
    scale = HEAD_DIM ** (-0.5)
    normed_in, norm_one, inverse_one = layer_norm(rows, gain_before, shift_before)
    query = (matmul(normed_in, query_matrix) + query_offset.astype(jnp.float32)).astype(jnp.bfloat16)
    keys = matmul(normed_in, key_matrix).astype(jnp.bfloat16)
    values = (matmul(normed_in, value_matrix) + value_offset.astype(jnp.float32)).astype(jnp.bfloat16)
    query_heads = query.astype(jnp.float32).reshape(FRAMES, HEADS, HEAD_DIM)
    key_heads = keys.astype(jnp.float32).reshape(FRAMES, HEADS, HEAD_DIM)
    value_heads = values.astype(jnp.float32).reshape(FRAMES, HEADS, HEAD_DIM)
    position = jnp.arange(FRAMES, dtype=jnp.int32)
    valid = (position < length)[None, None, :]
    scores = jnp.einsum('qhd,khd->hqk', query_heads, key_heads) * scale
    scores = jnp.where(valid, scores, NEG)
    highest = lax.optimization_barrier(jnp.max(scores, axis=-1, keepdims=True))
    expo = jnp.exp(scores - highest)
    total = lax.optimization_barrier(jnp.sum(expo, axis=-1, keepdims=True))
    logsum = highest + jnp.log(total)
    probs = jnp.exp(scores - logsum)
    probs_low = probs.astype(jnp.bfloat16).astype(jnp.float32)
    attended_heads = jnp.einsum('hqk,khd->qhd', probs_low, value_heads)
    attended = attended_heads.reshape(FRAMES, D).astype(jnp.bfloat16)
    middle = rows + matmul(attended, output_matrix) + output_offset.astype(jnp.float32)
    normed_mid, norm_two, inverse_two = layer_norm(middle, gain_middle, shift_middle)
    pre = matmul(normed_mid, up_matrix) + up_offset.astype(jnp.float32)
    hidden = gelu_value(pre).astype(jnp.bfloat16)
    block_out = middle + matmul(hidden, down_matrix) + down_offset.astype(jnp.float32)
    grad_low = upstream.astype(jnp.bfloat16)
    down_grad = outer_sum(hidden, grad_low)
    down_offset_grad = lax.optimization_barrier(jnp.sum(upstream, axis=0))
    pre_grad = back_matmul(grad_low, down_matrix) * gelu_slope(pre)
    pre_low = pre_grad.astype(jnp.bfloat16)
    up_grad = outer_sum(normed_mid, pre_low)
    up_offset_grad = lax.optimization_barrier(jnp.sum(pre_grad, axis=0))
    middle_part, gain_middle_grad, shift_middle_grad = norm_backward(back_matmul(pre_low, up_matrix), norm_two, inverse_two, gain_middle)
    middle_grad = upstream + middle_part
    middle_low = middle_grad.astype(jnp.bfloat16)
    output_grad = outer_sum(attended, middle_low)
    output_offset_grad = lax.optimization_barrier(jnp.sum(middle_grad, axis=0))
    attended_grad = back_matmul(middle_low, output_matrix).astype(jnp.bfloat16)
    grad_heads = attended_grad.astype(jnp.float32).reshape(FRAMES, HEADS, HEAD_DIM)
    prob_grad = jnp.einsum('qhd,khd->hqk', grad_heads, value_heads)
    delta = jnp.einsum('qhd,qhd->hq', grad_heads, attended.astype(jnp.float32).reshape(FRAMES, HEADS, HEAD_DIM))
    score_low = (probs * (prob_grad - delta[:, :, None]) * scale).astype(jnp.bfloat16).astype(jnp.float32)
    query_grad = jnp.einsum('hqk,khd->qhd', score_low, key_heads).reshape(FRAMES, D)
    key_grad = jnp.einsum('hqk,qhd->khd', score_low, query_heads).reshape(FRAMES, D)
    value_grad = jnp.einsum('hqk,qhd->khd', probs_low, grad_heads).reshape(FRAMES, D)
    query_low = query_grad.astype(jnp.bfloat16)
    key_low = key_grad.astype(jnp.bfloat16)
    value_low = value_grad.astype(jnp.bfloat16)
    query_matrix_grad = outer_sum(normed_in, query_low)
    key_matrix_grad = outer_sum(normed_in, key_low)
    value_matrix_grad = outer_sum(normed_in, value_low)
    query_offset_grad = lax.optimization_barrier(jnp.sum(query_grad, axis=0))
    value_offset_grad = lax.optimization_barrier(jnp.sum(value_grad, axis=0))
    upstream_in = back_matmul(query_low, query_matrix) + back_matmul(key_low, key_matrix) + back_matmul(value_low, value_matrix)
    input_part, gain_before_grad, shift_before_grad = norm_backward(upstream_in, norm_one, inverse_one, gain_before)
    input_grad = middle_grad + input_part
    grads = (gain_before_grad, shift_before_grad, query_matrix_grad, query_offset_grad, key_matrix_grad, value_matrix_grad, value_offset_grad, output_grad, output_offset_grad, gain_middle_grad, shift_middle_grad, up_grad, up_offset_grad, down_grad, down_offset_grad)
    return (block_out, input_grad, grads)

def reference(inputs, clip_lengths, first_gain, first_shift, query_weight, query_bias, key_weight, value_weight, value_bias, output_weight, output_bias, second_gain, second_shift, up_weight, up_bias, down_weight, down_bias, out_grad):
    params = (first_gain, first_shift, query_weight, query_bias, key_weight, value_weight, value_bias, output_weight, output_bias, second_gain, second_shift, up_weight, up_bias, down_weight, down_bias)
    initial = tuple((jnp.zeros(weight.shape, jnp.float32) for weight in params))

    def advance(carry, packed):
        rows, upstream, length = packed
        block_out, input_grad, grads = clip_pass(params, rows, upstream, length)
        summed = tuple((left + right for left, right in zip(carry, grads)))
        return (summed, (block_out, input_grad))
    totals, (block_out, input_grad) = lax.scan(advance, initial, (inputs, out_grad, clip_lengths))
    return (block_out, input_grad, totals[0], totals[1], totals[2], totals[3], totals[4], totals[5], totals[6], totals[7], totals[8], totals[9], totals[10], totals[11], totals[12], totals[13], totals[14])
```

```python
import functools

import jax
import jax.numpy as jnp
from jax import lax
from jax.sharding import PartitionSpec as P

HEADS = 12


EPS = 1e-05
NEG = -1e30
SQRT_HALF = 0.7071067811865476
INV_ROOT_TWO_PI = 0.3989422804014327


def layer_norm(rows, gain, shift):
    average = jnp.mean(rows, axis=-1, keepdims=True)
    centered = rows - average
    inverse = lax.rsqrt(jnp.mean(centered * centered, axis=-1, keepdims=True) + EPS)
    normed = centered * inverse
    result = normed * gain.astype(jnp.float32) + shift.astype(jnp.float32)
    return (result.astype(jnp.bfloat16), normed, inverse)


def norm_backward(upstream, normed, inverse, gain):
    scaled = upstream * gain.astype(jnp.float32)
    result = inverse * (
        scaled
        - jnp.mean(scaled, axis=-1, keepdims=True)
        - normed * jnp.mean(scaled * normed, axis=-1, keepdims=True)
    )
    return (result, jnp.sum(upstream * normed, axis=(0, 1)), jnp.sum(upstream, axis=(0, 1)))


def gelu_value(pre):
    return 0.5 * pre * (1.0 + lax.erf(pre * SQRT_HALF))


def gelu_slope(pre):
    return (
        0.5 * (1.0 + lax.erf(pre * SQRT_HALF)) + pre * jnp.exp(-0.5 * pre * pre) * INV_ROOT_TWO_PI
    )


def matmul(left, right):
    return jnp.dot(left, right, preferred_element_type=jnp.float32)


def back_matmul(left, right):
    return lax.dot_general(
        left, right, (((2,), (1,)), ((), ())), preferred_element_type=jnp.float32
    )


def outer_sum(left, right):
    return lax.dot_general(
        left, right, (((0, 1), (0, 1)), ((), ())), preferred_element_type=jnp.float32
    )


def split_heads(array):
    return array.reshape(array.shape[0], array.shape[1], HEADS, array.shape[2] // HEADS)


def masked_scores(query, keys, lengths, position):
    scale = (query.shape[2] // HEADS) ** (-0.5)
    scores = (
        jnp.einsum(
            "cqhd,ckhd->chqk",
            split_heads(query),
            split_heads(keys),
            preferred_element_type=jnp.float32,
        )
        * scale
    )
    valid = position[None, None, None, :] < lengths[:, None, None, None]
    return jnp.where(valid, scores, NEG)


def attention_forward(query, keys, values, lengths, position):
    scores = masked_scores(query, keys, lengths, position)
    highest = jnp.max(scores, axis=-1, keepdims=True)
    expo = jnp.exp(scores - highest)
    total = jnp.sum(expo, axis=-1, keepdims=True)
    logsum = highest + jnp.log(total)
    probs_low = (expo / total).astype(jnp.bfloat16)
    attended = jnp.einsum(
        "chqk,ckhd->cqhd", probs_low, split_heads(values), preferred_element_type=jnp.float32
    )
    return (attended.reshape(query.shape).astype(jnp.bfloat16), logsum)


def attention_backward(query, keys, values, attended, attended_grad, logsum, lengths, position):
    scale = (query.shape[2] // HEADS) ** (-0.5)
    probs = jnp.exp(masked_scores(query, keys, lengths, position) - logsum)
    probs_low = probs.astype(jnp.bfloat16)
    grad_heads = split_heads(attended_grad)
    prob_grad = jnp.einsum(
        "cqhd,ckhd->chqk", grad_heads, split_heads(values), preferred_element_type=jnp.float32
    )
    delta = jnp.einsum(
        "cqhd,cqhd->chq", grad_heads.astype(jnp.float32), split_heads(attended).astype(jnp.float32)
    )
    score_low = (probs * (prob_grad - delta[..., None]) * scale).astype(jnp.bfloat16)
    query_grad = jnp.einsum(
        "chqk,ckhd->cqhd", score_low, split_heads(keys), preferred_element_type=jnp.float32
    )
    key_part = jnp.einsum(
        "chqk,cqhd->ckhd", score_low, split_heads(query), preferred_element_type=jnp.float32
    )
    value_part = jnp.einsum(
        "chqk,cqhd->ckhd", probs_low, grad_heads, preferred_element_type=jnp.float32
    )
    return (
        query_grad.reshape(query.shape),
        key_part.reshape(keys.shape),
        value_part.reshape(keys.shape),
    )


def shift_from(array, axis, size, step):
    return lax.ppermute(array, axis, [((i + step) % size, i) for i in range(size)])


def gather_turned(own, axis, size, dim):
    blocks = [own] + [shift_from(own, axis, size, step) for step in range(1, size)]
    return jnp.concatenate(blocks, axis=dim)


def turn(array, size, dim, index):
    extent = array.shape[dim]
    if size == 2:
        low, high = jnp.split(array, 2, axis=dim)
        flipped = jnp.concatenate([high, low], axis=dim)
        return jnp.where(index == 0, array, flipped)
    twice = jnp.concatenate([array, array], axis=dim)
    return lax.dynamic_slice_in_dim(twice, index * (extent // size), extent, axis=dim)


def scatter_sum(block_of, axis, size):
    total = None
    for step in range(1, size):
        sent = block_of(step).astype(jnp.bfloat16)
        taken = shift_from(sent, axis, size, size - step).astype(jnp.float32)
        total = taken if total is None else total + taken
    own = block_of(0)
    return own if total is None else own + total


def swap_bit(array, axis, size, bit):
    return lax.ppermute(array, axis, [(i, i ^ (1 << bit)) for i in range(size)])


def halving_sum(block, axis, size, order):
    index = lax.axis_index(axis)
    for bit in order:
        half = block.shape[0] // 2
        mine = (index >> bit) & 1
        sent = lax.dynamic_slice_in_dim(block, (1 - mine) * half, half, axis=0)
        kept = lax.dynamic_slice_in_dim(block, mine * half, half, axis=0)
        taken = swap_bit(sent, axis, size, bit)
        block = (kept.astype(jnp.float32) + taken.astype(jnp.float32)).astype(jnp.bfloat16)
    for bit in reversed(order):
        mine = (index >> bit) & 1
        taken = swap_bit(block, axis, size, bit)
        first = jnp.where(mine == 0, block, taken)
        second = jnp.where(mine == 0, taken, block)
        block = jnp.concatenate([first, second], axis=0)
    return block


def bit_orders(size):
    bits = list(range(size.bit_length() - 1))
    if len(bits) == 4:
        return ([0, 1, 2, 3], [1, 0, 3, 2], [2, 3, 0, 1])
    return tuple(bits[k:] + bits[:k] for k in range(3))


def sum_rows(stacked, axis, size):
    third = stacked.shape[0] // 3
    return jnp.concatenate(
        [
            halving_sum(stacked[k * third : (k + 1) * third], axis, size, order)
            for k, order in enumerate(bit_orders(size))
        ],
        axis=0,
    )


def doubling_sum(array, axis, size):
    for bit in range(size.bit_length() - 1):
        array = array + swap_bit(array, axis, size, bit)
    return array


def on_device(
    reps,
    grps,
    inputs,
    clip_lengths,
    first_gain,
    first_shift,
    query_weight,
    query_bias,
    key_weight,
    value_weight,
    value_bias,
    output_weight,
    output_bias,
    second_gain,
    second_shift,
    up_weight,
    up_bias,
    down_weight,
    down_bias,
    out_grad,
):
    core = lax.axis_index("grp")
    vectors = (
        first_gain,
        first_shift,
        query_bias,
        value_bias,
        output_bias,
        second_gain,
        second_shift,
        down_bias,
        up_bias,
    )
    packed = lax.all_gather(jnp.concatenate(vectors), "grp", axis=0, tiled=False)
    unpacked, at = [], 0
    for vector in vectors:
        unpacked.append(packed[:, at : at + vector.shape[0]].reshape(-1))
        at += vector.shape[0]
    (
        gain_before,
        shift_before,
        query_offset,
        value_offset,
        output_offset,
        gain_middle,
        shift_middle,
        down_offset,
        up_offset,
    ) = unpacked
    key_matrix = gather_turned(key_weight, "grp", grps, 0)
    value_matrix = gather_turned(value_weight, "grp", grps, 0)
    query_matrix = gather_turned(query_weight, "grp", grps, 0)
    output_matrix = lax.all_gather(output_weight, "grp", axis=0, tiled=True)
    up_matrix = lax.all_gather(up_weight, "grp", axis=0, tiled=True)
    down_matrix = lax.all_gather(down_weight, "grp", axis=0, tiled=True)
    width = first_gain.shape[0]
    wide = up_bias.shape[0]
    frames = inputs.shape[1]

    normed_in, norm_one, inverse_one = layer_norm(inputs, gain_before, shift_before)
    turned = turn(normed_in, grps, 2, core)
    keys = matmul(turned, key_matrix).astype(jnp.bfloat16)
    values = (matmul(turned, value_matrix) + value_offset.astype(jnp.float32)).astype(
        jnp.bfloat16
    )
    all_keys = gather_turned(keys, "grp", grps, 1)
    all_values = gather_turned(values, "grp", grps, 1)
    query = (matmul(turned, query_matrix) + query_offset.astype(jnp.float32)).astype(
        jnp.bfloat16
    )
    slot = lax.iota(jnp.int32, grps * frames)
    position = lax.rem(slot + core * frames, grps * frames)
    attended, logsum = attention_forward(query, all_keys, all_values, clip_lengths, position)
    middle = inputs + matmul(attended, output_matrix) + output_offset.astype(jnp.float32)
    normed_mid, norm_two, inverse_two = layer_norm(middle, gain_middle, shift_middle)
    pre = matmul(normed_mid, up_matrix) + up_offset.astype(jnp.float32)
    hidden = gelu_value(pre).astype(jnp.bfloat16)
    block_out = middle + matmul(hidden, down_matrix) + down_offset.astype(jnp.float32)

    def columns(array, step, extent):
        start = lax.rem(core + step, grps) * extent
        return lax.dynamic_slice_in_dim(array, start, extent, axis=2)

    grad_low = out_grad.astype(jnp.bfloat16)
    down_grad = scatter_sum(
        lambda step: outer_sum(columns(hidden, step, wide), grad_low), "grp", grps
    )
    down_offset_grad = jnp.sum(out_grad, axis=(0, 1))
    pre_grad = back_matmul(grad_low, down_matrix) * gelu_slope(pre)
    pre_low = pre_grad.astype(jnp.bfloat16)
    up_grad = scatter_sum(
        lambda step: outer_sum(columns(normed_mid, step, width), pre_low), "grp", grps
    )
    full = down_weight.shape[1]
    pieces = up_grad.shape[1] // full
    stacked = jnp.concatenate(
        [down_grad.astype(jnp.bfloat16)]
        + [up_grad[:, k * full : (k + 1) * full].astype(jnp.bfloat16) for k in range(pieces)],
        axis=0,
    )
    early = sum_rows(stacked, "rep", reps)
    up_offset_grad = jnp.sum(pre_grad, axis=(0, 1))
    middle_part, gain_middle_grad, shift_middle_grad = norm_backward(
        back_matmul(pre_low, up_matrix), norm_two, inverse_two, gain_middle
    )
    middle_grad = out_grad + middle_part
    middle_low = middle_grad.astype(jnp.bfloat16)
    output_grad = scatter_sum(
        lambda step: outer_sum(columns(attended, step, width), middle_low), "grp", grps
    )
    output_offset_grad = jnp.sum(middle_grad, axis=(0, 1))
    attended_grad = back_matmul(middle_low, output_matrix).astype(jnp.bfloat16)
    query_grad, key_part, value_part = attention_backward(
        query, all_keys, all_values, attended, attended_grad, logsum, clip_lengths, position
    )
    value_grad = scatter_sum(
        lambda step: value_part[:, step * frames : (step + 1) * frames], "grp", grps
    )
    key_grad = scatter_sum(
        lambda step: key_part[:, step * frames : (step + 1) * frames], "grp", grps
    )
    query_low = query_grad.astype(jnp.bfloat16)
    key_low = key_grad.astype(jnp.bfloat16)
    value_low = value_grad.astype(jnp.bfloat16)

    def turned_outer(low):
        return scatter_sum(
            lambda step: outer_sum(turned[:, :, step * width : (step + 1) * width], low),
            "grp",
            grps,
        )

    query_matrix_grad = turned_outer(query_low)
    value_matrix_grad = turned_outer(value_low)
    key_matrix_grad = turned_outer(key_low)
    late = sum_rows(
        jnp.concatenate(
            [
                grad.astype(jnp.bfloat16)
                for grad in (output_grad, query_matrix_grad, value_matrix_grad, key_matrix_grad)
            ],
            axis=0,
        ),
        "rep",
        reps,
    )
    query_offset_grad = jnp.sum(query_grad, axis=(0, 1))
    value_offset_grad = jnp.sum(value_grad, axis=(0, 1))
    upstream_in = turn(
        back_matmul(query_low, query_matrix)
        + back_matmul(key_low, key_matrix)
        + back_matmul(value_low, value_matrix),
        grps,
        2,
        lax.rem(grps - core, grps),
    )
    input_part, gain_before_grad, shift_before_grad = norm_backward(
        upstream_in, norm_one, inverse_one, gain_before
    )
    input_grad = middle_grad + input_part

    summed = jnp.concatenate(
        [
            grad.reshape(grps, -1)
            for grad in (
                gain_before_grad,
                shift_before_grad,
                query_offset_grad,
                value_offset_grad,
                output_offset_grad,
                gain_middle_grad,
                shift_middle_grad,
                down_offset_grad,
                up_offset_grad,
            )
        ],
        axis=1,
    )
    summed = scatter_sum(
        lambda step: lax.dynamic_index_in_dim(
            summed, lax.rem(core + step, grps), 0, keepdims=False
        ).reshape(-1, 128),
        "grp",
        grps,
    )
    summed = doubling_sum(summed, "rep", reps).reshape(-1)

    def vector(k):
        return summed[k * width : (k + 1) * width]

    late = late.astype(jnp.float32)
    early = early.astype(jnp.float32)
    up_rows = early[wide:]
    return (
        block_out,
        input_grad,
        vector(0),
        vector(1),
        late[width : 2 * width],
        vector(2),
        late[3 * width :],
        late[2 * width : 3 * width],
        vector(3),
        late[:width],
        vector(4),
        vector(5),
        vector(6),
        jnp.concatenate([up_rows[k * width : (k + 1) * width] for k in range(pieces)], axis=1),
        summed[8 * width :],
        early[:wide],
        vector(7),
    )


def solution(mesh):
    return jax.shard_map(
        functools.partial(on_device, mesh.shape["rep"], mesh.shape["grp"]),
        mesh=mesh,
        in_specs=(
            P("rep", "grp", None),
            P("rep"),
            P("grp"),
            P("grp"),
            P("grp", None),
            P("grp"),
            P("grp", None),
            P("grp", None),
            P("grp"),
            P("grp", None),
            P("grp"),
            P("grp"),
            P("grp"),
            P("grp", None),
            P("grp"),
            P("grp", None),
            P("grp"),
            P("rep", "grp", None),
        ),
        out_specs=(
            P("rep", "grp", None),
            P("rep", "grp", None),
            P("grp"),
            P("grp"),
            P("grp", None),
            P("grp"),
            P("grp", None),
            P("grp", None),
            P("grp"),
            P("grp", None),
            P("grp"),
            P("grp"),
            P("grp"),
            P("grp", None),
            P("grp"),
            P("grp", None),
            P("grp"),
        ),
        check_vma=False,
    )
```

```python
import functools

import jax
import jax.numpy as jnp
from jax import lax
from jax.experimental import pallas as pl
from jax.experimental.pallas import tpu as pltpu
from jax.sharding import PartitionSpec as P

HEADS = 12


EPS = 1e-05
NEG = -1e30
SQRT_HALF = 0.7071067811865476
INV_ROOT_TWO_PI = 0.3989422804014327


def layer_norm(rows, gain, shift):
    average = jnp.mean(rows, axis=-1, keepdims=True)
    centered = rows - average
    inverse = lax.rsqrt(jnp.mean(centered * centered, axis=-1, keepdims=True) + EPS)
    normed = centered * inverse
    result = normed * gain.astype(jnp.float32) + shift.astype(jnp.float32)
    return (result.astype(jnp.bfloat16), normed, inverse)


def norm_backward(upstream, normed, inverse, gain):
    scaled = upstream * gain.astype(jnp.float32)
    result = inverse * (
        scaled
        - jnp.mean(scaled, axis=-1, keepdims=True)
        - normed * jnp.mean(scaled * normed, axis=-1, keepdims=True)
    )
    return (result, jnp.sum(upstream * normed, axis=(0, 1)), jnp.sum(upstream, axis=(0, 1)))


def gelu_value(pre):
    return 0.5 * pre * (1.0 + lax.erf(pre * SQRT_HALF))


def gelu_slope(pre):
    return (
        0.5 * (1.0 + lax.erf(pre * SQRT_HALF)) + pre * jnp.exp(-0.5 * pre * pre) * INV_ROOT_TWO_PI
    )


def matmul(left, right):
    return jnp.dot(left, right, preferred_element_type=jnp.float32)


def back_matmul(left, right):
    return lax.dot_general(
        left, right, (((2,), (1,)), ((), ())), preferred_element_type=jnp.float32
    )


def outer_sum(left, right):
    return lax.dot_general(
        left, right, (((0, 1), (0, 1)), ((), ())), preferred_element_type=jnp.float32
    )


def scores_of(keys, query, valid, scale):
    scores = lax.dot_general(
        keys, query, (((1,), (1,)), ((), ())), preferred_element_type=jnp.float32
    )
    return jnp.where(valid > 0.0, scores * scale, NEG)


def across(left, right):
    return lax.dot_general(
        left, right, (((0,), (0,)), ((), ())), preferred_element_type=jnp.float32
    )


def forward_kernel(size, query_ref, keys_ref, values_ref, valid_ref, attended_ref, logsum_ref):
    valid = valid_ref[...]
    parts = []
    for head in range(2):
        at = slice(head * size, (head + 1) * size)
        scores = scores_of(keys_ref[:, at], query_ref[:, at], valid, size ** (-0.5))
        highest = jnp.max(scores, axis=0, keepdims=True)
        expo = jnp.exp(scores - highest)
        total = jnp.sum(expo, axis=0, keepdims=True)
        probs_low = (expo * (1.0 / total)).astype(jnp.bfloat16)
        parts.append(across(values_ref[:, at], probs_low))
        logsum_ref[0, head : head + 1, :] = highest + jnp.log(total)
    attended_ref[...] = jnp.concatenate(parts, axis=0).T.astype(jnp.bfloat16)


def backward_kernel(
    size,
    query_ref,
    keys_ref,
    values_ref,
    attended_ref,
    upstream_ref,
    logsum_ref,
    valid_ref,
    query_out,
    keys_out,
    values_out,
):
    valid = valid_ref[...]
    scale = size ** (-0.5)
    product = upstream_ref[...].astype(jnp.float32) * attended_ref[...].astype(jnp.float32)
    product = product.T
    query_parts, key_parts, value_parts = [], [], []
    for head in range(2):
        at = slice(head * size, (head + 1) * size)
        query, keys, upstream = query_ref[:, at], keys_ref[:, at], upstream_ref[:, at]
        delta = jnp.sum(product[at], axis=0, keepdims=True)
        scores = scores_of(keys, query, valid, scale)
        probs = jnp.exp(scores - logsum_ref[0, head : head + 1, :])
        prob_grad = lax.dot_general(
            values_ref[:, at], upstream, (((1,), (1,)), ((), ())),
            preferred_element_type=jnp.float32,
        )
        score_low = (probs * (prob_grad - delta) * scale).astype(jnp.bfloat16)
        query_parts.append(across(keys, score_low))
        key_parts.append(matmul(score_low, query))
        value_parts.append(matmul(probs.astype(jnp.bfloat16), upstream))
    query_out[...] = jnp.concatenate(query_parts, axis=0).T
    keys_out[...] = jnp.concatenate(key_parts, axis=1).astype(jnp.bfloat16)
    values_out[...] = jnp.concatenate(value_parts, axis=1).astype(jnp.bfloat16)


PAIRS = HEADS // 2


def attention_forward(query, keys, values, valid):
    rows, full = query.shape
    span = keys.shape[0]
    pair = full // PAIRS
    mine = pl.BlockSpec((rows, pair), lambda i: (0, i))
    every = pl.BlockSpec((span, pair), lambda i: (0, i))
    return pl.pallas_call(
        functools.partial(forward_kernel, pair // 2),
        grid=(PAIRS,),
        in_specs=[mine, every, every, pl.BlockSpec((span, 1), lambda i: (0, 0))],
        out_specs=[mine, pl.BlockSpec((1, 2, rows), lambda i: (i, 0, 0))],
        out_shape=[
            jax.ShapeDtypeStruct((rows, full), jnp.bfloat16),
            jax.ShapeDtypeStruct((PAIRS, 2, rows), jnp.float32),
        ],
        cost_estimate=pl.CostEstimate(
            flops=16 * rows * span * full, bytes_accessed=8 * span * full, transcendentals=0
        ),
        compiler_params=pltpu.CompilerParams(vmem_limit_bytes=48 * 2**20),
    )(query, keys, values, valid)


def attention_backward(query, keys, values, attended, upstream, logsum, valid, first, count):
    rows, full = query.shape
    span = keys.shape[0]
    pair = full // PAIRS
    mine = pl.BlockSpec((rows, pair), lambda i: (0, i + first))
    every = pl.BlockSpec((span, pair), lambda i: (0, i + first))
    return pl.pallas_call(
        functools.partial(backward_kernel, pair // 2),
        grid=(count,),
        in_specs=[
            mine,
            every,
            every,
            mine,
            mine,
            pl.BlockSpec((1, 2, rows), lambda i: (i + first, 0, 0)),
            pl.BlockSpec((span, 1), lambda i: (0, 0)),
        ],
        out_specs=[
            pl.BlockSpec((rows, pair), lambda i: (0, i)),
            pl.BlockSpec((span, pair), lambda i: (0, i)),
            pl.BlockSpec((span, pair), lambda i: (0, i)),
        ],
        out_shape=[
            jax.ShapeDtypeStruct((rows, count * pair), jnp.float32),
            jax.ShapeDtypeStruct((span, count * pair), jnp.bfloat16),
            jax.ShapeDtypeStruct((span, count * pair), jnp.bfloat16),
        ],
        cost_estimate=pl.CostEstimate(
            flops=40 * rows * span * count * pair,
            bytes_accessed=16 * span * count * pair,
            transcendentals=0,
        ),
        compiler_params=pltpu.CompilerParams(vmem_limit_bytes=48 * 2**20),
    )(query, keys, values, attended, upstream, logsum, valid)


def shift_from(array, axis, size, step):
    return lax.ppermute(array, axis, [((i + step) % size, i) for i in range(size)])


def gather_turned(own, axis, size, dim):
    blocks = [own] + [shift_from(own, axis, size, step) for step in range(1, size)]
    return jnp.concatenate(blocks, axis=dim)


def turn(array, size, dim, index):
    extent = array.shape[dim]
    if size == 2:
        low, high = jnp.split(array, 2, axis=dim)
        flipped = jnp.concatenate([high, low], axis=dim)
        return jnp.where(index == 0, array, flipped)
    twice = jnp.concatenate([array, array], axis=dim)
    return lax.dynamic_slice_in_dim(twice, index * (extent // size), extent, axis=dim)


def scatter_sum(block_of, axis, size):
    total = None
    for step in range(1, size):
        sent = block_of(step).astype(jnp.bfloat16)
        taken = shift_from(sent, axis, size, size - step).astype(jnp.float32)
        total = taken if total is None else total + taken
    own = block_of(0).astype(jnp.float32)
    return own if total is None else own + total


def swap_bit(array, axis, size, bit):
    return lax.ppermute(array, axis, [(i, i ^ (1 << bit)) for i in range(size)])


def halve(block, axis, size, bit):
    half = block.shape[0] // 2
    mine = (lax.axis_index(axis) >> bit) & 1
    sent = lax.dynamic_slice_in_dim(block, (1 - mine) * half, half, axis=0)
    kept = lax.dynamic_slice_in_dim(block, mine * half, half, axis=0)
    taken = swap_bit(sent, axis, size, bit)
    return (kept.astype(jnp.float32) + taken.astype(jnp.float32)).astype(jnp.bfloat16)


def double(block, axis, size, bit):
    mine = (lax.axis_index(axis) >> bit) & 1
    taken = swap_bit(block, axis, size, bit)
    first = jnp.where(mine == 0, block, taken)
    second = jnp.where(mine == 0, taken, block)
    return jnp.concatenate([first, second], axis=0)


def bit_orders(size):
    bits = list(range(size.bit_length() - 1))
    if len(bits) == 4:
        return ([0, 1, 2, 3], [1, 0, 3, 2], [2, 3, 0, 1])
    return tuple(bits[k:] + bits[:k] for k in range(3))


def sum_steps(size):
    orders = bit_orders(size)
    steps = [(halve, [order[k] for order in orders]) for k in range(len(orders[0]))]
    return steps + [(double, bits) for _, bits in reversed(steps)]


def thirds(stacked):
    return list(jnp.split(stacked, 3, axis=0))


def advance(blocks, axis, size, steps):
    for move, bits in steps:
        blocks = [move(block, axis, size, bit) for block, bit in zip(blocks, bits)]
    return blocks


def doubling_sum(array, axis, size):
    for bit in range(size.bit_length() - 1):
        array = array + swap_bit(array, axis, size, bit)
    return array


def on_device(
    reps,
    grps,
    inputs,
    clip_lengths,
    first_gain,
    first_shift,
    query_weight,
    query_bias,
    key_weight,
    value_weight,
    value_bias,
    output_weight,
    output_bias,
    second_gain,
    second_shift,
    up_weight,
    up_bias,
    down_weight,
    down_bias,
    out_grad,
):
    core = lax.axis_index("grp")
    vectors = (
        first_gain,
        first_shift,
        query_bias,
        value_bias,
        output_bias,
        second_gain,
        second_shift,
        down_bias,
        up_bias,
    )
    packed = lax.all_gather(jnp.concatenate(vectors), "grp", axis=0, tiled=False)
    unpacked, at = [], 0
    for vector in vectors:
        unpacked.append(packed[:, at : at + vector.shape[0]].reshape(-1))
        at += vector.shape[0]
    (
        gain_before,
        shift_before,
        query_offset,
        value_offset,
        output_offset,
        gain_middle,
        shift_middle,
        down_offset,
        up_offset,
    ) = unpacked
    key_matrix = gather_turned(key_weight, "grp", grps, 0)
    value_matrix = gather_turned(value_weight, "grp", grps, 0)
    query_matrix = gather_turned(query_weight, "grp", grps, 0)
    output_matrix = lax.all_gather(output_weight, "grp", axis=0, tiled=True)
    up_matrix = lax.all_gather(up_weight, "grp", axis=0, tiled=True)
    down_matrix = lax.all_gather(down_weight, "grp", axis=0, tiled=True)
    width = first_gain.shape[0]
    wide = up_bias.shape[0]
    frames = inputs.shape[1]

    normed_in, norm_one, inverse_one = layer_norm(inputs, gain_before, shift_before)
    turned = turn(normed_in, grps, 2, core)
    keys = matmul(turned, key_matrix).astype(jnp.bfloat16)
    values = (matmul(turned, value_matrix) + value_offset.astype(jnp.float32)).astype(
        jnp.bfloat16
    )
    all_keys = gather_turned(keys, "grp", grps, 1)
    all_values = gather_turned(values, "grp", grps, 1)
    query = (matmul(turned, query_matrix) + query_offset.astype(jnp.float32)).astype(
        jnp.bfloat16
    )
    slot = lax.iota(jnp.int32, grps * frames)
    position = lax.rem(slot + core * frames, grps * frames)
    valid = (position < clip_lengths[0]).astype(jnp.float32)[:, None]
    attended, logsum = attention_forward(query[0], all_keys[0], all_values[0], valid)
    attended = attended[None]
    middle = inputs + matmul(attended, output_matrix) + output_offset.astype(jnp.float32)
    normed_mid, norm_two, inverse_two = layer_norm(middle, gain_middle, shift_middle)
    pre = matmul(normed_mid, up_matrix) + up_offset.astype(jnp.float32)
    hidden = gelu_value(pre).astype(jnp.bfloat16)
    block_out = middle + matmul(hidden, down_matrix) + down_offset.astype(jnp.float32)

    def columns(array, step, extent):
        start = lax.rem(core + step, grps) * extent
        return lax.dynamic_slice_in_dim(array, start, extent, axis=2)

    grad_low = out_grad.astype(jnp.bfloat16)
    down_grad = scatter_sum(
        lambda step: outer_sum(columns(hidden, step, wide), grad_low), "grp", grps
    )
    down_offset_grad = jnp.sum(out_grad, axis=(0, 1))
    pre_grad = back_matmul(grad_low, down_matrix) * gelu_slope(pre)
    pre_low = pre_grad.astype(jnp.bfloat16)
    up_grad = scatter_sum(
        lambda step: outer_sum(columns(normed_mid, step, width), pre_low), "grp", grps
    )
    full = down_weight.shape[1]
    pieces = up_grad.shape[1] // full
    stacked = jnp.concatenate(
        [down_grad.astype(jnp.bfloat16)]
        + [up_grad[:, k * full : (k + 1) * full].astype(jnp.bfloat16) for k in range(pieces)],
        axis=0,
    )
    early = thirds(stacked)
    up_offset_grad = jnp.sum(pre_grad, axis=(0, 1))
    middle_part, gain_middle_grad, shift_middle_grad = norm_backward(
        back_matmul(pre_low, up_matrix), norm_two, inverse_two, gain_middle
    )
    middle_grad = out_grad + middle_part
    middle_low = middle_grad.astype(jnp.bfloat16)
    output_grad = scatter_sum(
        lambda step: outer_sum(columns(attended, step, width), middle_low), "grp", grps
    )
    output_offset_grad = jnp.sum(middle_grad, axis=(0, 1))
    attended_grad = back_matmul(middle_low, output_matrix).astype(jnp.bfloat16)
    steps = sum_steps(reps)
    bits = len(steps) // 2
    early, attended_grad = lax.optimization_barrier((early, attended_grad))
    stages = (steps[:1], steps[1:2], steps[2:bits])
    parts = []
    count = PAIRS // len(stages)
    for stage, moves in enumerate(stages):
        early = advance(early, "rep", reps, moves)
        part = attention_backward(
            query[0],
            all_keys[0],
            all_values[0],
            attended[0],
            attended_grad[0],
            logsum,
            valid,
            stage * count,
            count,
        )
        early, attended_grad, part = lax.optimization_barrier((early, attended_grad, part))
        parts.append(part)
    query_grad, key_part, value_part = (
        jnp.concatenate([part[k] for part in parts], axis=1)[None] for k in range(3)
    )
    early = advance(early, "rep", reps, steps[bits : 2 * bits - 2])
    value_grad = scatter_sum(
        lambda step: value_part[:, step * frames : (step + 1) * frames], "grp", grps
    )
    key_grad = scatter_sum(
        lambda step: key_part[:, step * frames : (step + 1) * frames], "grp", grps
    )
    query_grad, early = lax.optimization_barrier((query_grad, early))
    early = advance(early, "rep", reps, steps[2 * bits - 2 :])
    query_low = query_grad.astype(jnp.bfloat16)
    key_low = key_grad.astype(jnp.bfloat16)
    value_low = value_grad.astype(jnp.bfloat16)

    def turned_outer(low):
        return scatter_sum(
            lambda step: outer_sum(turned[:, :, step * width : (step + 1) * width], low),
            "grp",
            grps,
        )

    query_matrix_grad = turned_outer(query_low)
    value_matrix_grad = turned_outer(value_low)
    key_matrix_grad = turned_outer(key_low)
    late = jnp.concatenate(
        [
            grad.astype(jnp.bfloat16)
            for grad in (output_grad, query_matrix_grad, value_matrix_grad, key_matrix_grad)
        ],
        axis=0,
    )
    late = jnp.concatenate(advance(thirds(late), "rep", reps, steps), axis=0)
    query_offset_grad = jnp.sum(query_grad, axis=(0, 1))
    value_offset_grad = jnp.sum(value_grad, axis=(0, 1))
    upstream_in = turn(
        back_matmul(query_low, query_matrix)
        + back_matmul(key_low, key_matrix)
        + back_matmul(value_low, value_matrix),
        grps,
        2,
        lax.rem(grps - core, grps),
    )
    input_part, gain_before_grad, shift_before_grad = norm_backward(
        upstream_in, norm_one, inverse_one, gain_before
    )
    input_grad = middle_grad + input_part

    summed = jnp.concatenate(
        [
            grad.reshape(grps, -1)
            for grad in (
                gain_before_grad,
                shift_before_grad,
                query_offset_grad,
                value_offset_grad,
                output_offset_grad,
                gain_middle_grad,
                shift_middle_grad,
                down_offset_grad,
                up_offset_grad,
            )
        ],
        axis=1,
    )
    summed = scatter_sum(
        lambda step: lax.dynamic_index_in_dim(
            summed, lax.rem(core + step, grps), 0, keepdims=False
        ).reshape(-1, 128),
        "grp",
        grps,
    )
    summed = doubling_sum(summed, "rep", reps).reshape(-1)

    def vector(k):
        return summed[k * width : (k + 1) * width]

    late = late.astype(jnp.float32)
    early = jnp.concatenate(early, axis=0).astype(jnp.float32)
    up_rows = early[wide:]
    return (
        block_out,
        input_grad,
        vector(0),
        vector(1),
        late[width : 2 * width],
        vector(2),
        late[3 * width :],
        late[2 * width : 3 * width],
        vector(3),
        late[:width],
        vector(4),
        vector(5),
        vector(6),
        jnp.concatenate([up_rows[k * width : (k + 1) * width] for k in range(pieces)], axis=1),
        summed[8 * width :],
        early[:wide],
        vector(7),
    )


def solution(mesh):
    return jax.shard_map(
        functools.partial(on_device, mesh.shape["rep"], mesh.shape["grp"]),
        mesh=mesh,
        in_specs=(
            P("rep", "grp", None),
            P("rep"),
            P("grp"),
            P("grp"),
            P("grp", None),
            P("grp"),
            P("grp", None),
            P("grp", None),
            P("grp"),
            P("grp", None),
            P("grp"),
            P("grp"),
            P("grp"),
            P("grp", None),
            P("grp"),
            P("grp", None),
            P("grp"),
            P("rep", "grp", None),
        ),
        out_specs=(
            P("rep", "grp", None),
            P("rep", "grp", None),
            P("grp"),
            P("grp"),
            P("grp", None),
            P("grp"),
            P("grp", None),
            P("grp", None),
            P("grp"),
            P("grp", None),
            P("grp"),
            P("grp"),
            P("grp"),
            P("grp", None),
            P("grp"),
            P("grp", None),
            P("grp"),
        ),
        check_vma=False,
    )
```

```python
import functools

import jax
import jax.numpy as jnp
from jax import lax
from jax.experimental import pallas as pl
from jax.experimental.pallas import tpu as pltpu
from jax.sharding import PartitionSpec as P

HEADS = 12


EPS = 1e-05
NEG = -1e30
SQRT_HALF = 0.7071067811865476
INV_ROOT_TWO_PI = 0.3989422804014327


def layer_norm(rows, gain, shift):
    average = jnp.mean(rows, axis=-1, keepdims=True)
    centered = rows - average
    inverse = lax.rsqrt(jnp.mean(centered * centered, axis=-1, keepdims=True) + EPS)
    normed = centered * inverse
    result = normed * gain.astype(jnp.float32) + shift.astype(jnp.float32)
    return (result.astype(jnp.bfloat16), normed, inverse)


def norm_backward(upstream, normed, inverse, gain):
    scaled = upstream * gain.astype(jnp.float32)
    result = inverse * (
        scaled
        - jnp.mean(scaled, axis=-1, keepdims=True)
        - normed * jnp.mean(scaled * normed, axis=-1, keepdims=True)
    )
    return (result, jnp.sum(upstream * normed, axis=(0, 1)), jnp.sum(upstream, axis=(0, 1)))


def gelu_value(pre):
    return 0.5 * pre * (1.0 + lax.erf(pre * SQRT_HALF))


def gelu_slope(pre):
    return (
        0.5 * (1.0 + lax.erf(pre * SQRT_HALF)) + pre * jnp.exp(-0.5 * pre * pre) * INV_ROOT_TWO_PI
    )


def matmul(left, right):
    return jnp.dot(left, right, preferred_element_type=jnp.float32)


def back_matmul(left, right):
    return lax.dot_general(
        left, right, (((2,), (1,)), ((), ())), preferred_element_type=jnp.float32
    )


def outer_sum(left, right):
    return lax.dot_general(
        left, right, (((0, 1), (0, 1)), ((), ())), preferred_element_type=jnp.float32
    )


def scores_of(keys, query, valid, scale):
    scores = lax.dot_general(
        keys, query, (((1,), (1,)), ((), ())), preferred_element_type=jnp.float32
    )
    return jnp.where(valid > 0.0, scores * scale, NEG)


def across(left, right):
    return lax.dot_general(
        left, right, (((0,), (0,)), ((), ())), preferred_element_type=jnp.float32
    )


def forward_kernel(size, query_ref, keys_ref, values_ref, valid_ref, attended_ref, logsum_ref):
    valid = valid_ref[...]
    parts = []
    for head in range(2):
        at = slice(head * size, (head + 1) * size)
        scores = scores_of(keys_ref[:, at], query_ref[:, at], valid, size ** (-0.5))
        highest = jnp.max(scores, axis=0, keepdims=True)
        expo = jnp.exp(scores - highest)
        total = jnp.sum(expo, axis=0, keepdims=True)
        probs_low = (expo * (1.0 / total)).astype(jnp.bfloat16)
        parts.append(across(values_ref[:, at], probs_low))
        logsum_ref[0, head : head + 1, :] = highest + jnp.log(total)
    attended_ref[...] = jnp.concatenate(parts, axis=0).T.astype(jnp.bfloat16)


def backward_kernel(
    size,
    query_ref,
    keys_ref,
    values_ref,
    attended_ref,
    upstream_ref,
    logsum_ref,
    valid_ref,
    query_out,
    keys_out,
    values_out,
):
    valid = valid_ref[...]
    scale = size ** (-0.5)
    product = upstream_ref[...].astype(jnp.float32) * attended_ref[...].astype(jnp.float32)
    product = product.T
    query_parts, key_parts, value_parts = [], [], []
    for head in range(2):
        at = slice(head * size, (head + 1) * size)
        query, keys, upstream = query_ref[:, at], keys_ref[:, at], upstream_ref[:, at]
        delta = jnp.sum(product[at], axis=0, keepdims=True)
        scores = scores_of(keys, query, valid, scale)
        probs = jnp.exp(scores - logsum_ref[0, head : head + 1, :])
        prob_grad = lax.dot_general(
            values_ref[:, at], upstream, (((1,), (1,)), ((), ())),
            preferred_element_type=jnp.float32,
        )
        score_low = (probs * (prob_grad - delta) * scale).astype(jnp.bfloat16)
        query_parts.append(across(keys, score_low))
        key_parts.append(matmul(score_low, query))
        value_parts.append(matmul(probs.astype(jnp.bfloat16), upstream))
    query_out[...] = jnp.concatenate(query_parts, axis=0).T
    keys_out[...] = jnp.concatenate(key_parts, axis=1).astype(jnp.bfloat16)
    values_out[...] = jnp.concatenate(value_parts, axis=1).astype(jnp.bfloat16)


PAIRS = HEADS // 2


def attention_forward(query, keys, values, valid):
    rows, full = query.shape
    span = keys.shape[0]
    pair = full // PAIRS
    mine = pl.BlockSpec((rows, pair), lambda i: (0, i))
    every = pl.BlockSpec((span, pair), lambda i: (0, i))
    return pl.pallas_call(
        functools.partial(forward_kernel, pair // 2),
        grid=(PAIRS,),
        in_specs=[mine, every, every, pl.BlockSpec((span, 1), lambda i: (0, 0))],
        out_specs=[mine, pl.BlockSpec((1, 2, rows), lambda i: (i, 0, 0))],
        out_shape=[
            jax.ShapeDtypeStruct((rows, full), jnp.bfloat16),
            jax.ShapeDtypeStruct((PAIRS, 2, rows), jnp.float32),
        ],
        cost_estimate=pl.CostEstimate(
            flops=16 * rows * span * full, bytes_accessed=8 * span * full, transcendentals=0
        ),
        compiler_params=pltpu.CompilerParams(vmem_limit_bytes=48 * 2**20),
    )(query, keys, values, valid)


def attention_backward(query, keys, values, attended, upstream, logsum, valid, first, count):
    rows, full = query.shape
    span = keys.shape[0]
    pair = full // PAIRS
    mine = pl.BlockSpec((rows, pair), lambda i: (0, i + first))
    every = pl.BlockSpec((span, pair), lambda i: (0, i + first))
    return pl.pallas_call(
        functools.partial(backward_kernel, pair // 2),
        grid=(count,),
        in_specs=[
            mine,
            every,
            every,
            mine,
            mine,
            pl.BlockSpec((1, 2, rows), lambda i: (i + first, 0, 0)),
            pl.BlockSpec((span, 1), lambda i: (0, 0)),
        ],
        out_specs=[
            pl.BlockSpec((rows, pair), lambda i: (0, i)),
            pl.BlockSpec((span, pair), lambda i: (0, i)),
            pl.BlockSpec((span, pair), lambda i: (0, i)),
        ],
        out_shape=[
            jax.ShapeDtypeStruct((rows, count * pair), jnp.float32),
            jax.ShapeDtypeStruct((span, count * pair), jnp.bfloat16),
            jax.ShapeDtypeStruct((span, count * pair), jnp.bfloat16),
        ],
        cost_estimate=pl.CostEstimate(
            flops=40 * rows * span * count * pair,
            bytes_accessed=16 * span * count * pair,
            transcendentals=0,
        ),
        compiler_params=pltpu.CompilerParams(vmem_limit_bytes=48 * 2**20),
    )(query, keys, values, attended, upstream, logsum, valid)


def shift_from(array, axis, size, step):
    return lax.ppermute(array, axis, [((i + step) % size, i) for i in range(size)])


def gather_turned(own, axis, size, dim):
    blocks = [own] + [shift_from(own, axis, size, step) for step in range(1, size)]
    return jnp.concatenate(blocks, axis=dim)


def turn(array, size, dim, index):
    extent = array.shape[dim]
    if size == 2:
        low, high = jnp.split(array, 2, axis=dim)
        flipped = jnp.concatenate([high, low], axis=dim)
        return jnp.where(index == 0, array, flipped)
    twice = jnp.concatenate([array, array], axis=dim)
    return lax.dynamic_slice_in_dim(twice, index * (extent // size), extent, axis=dim)


def scatter_sum(block_of, axis, size):
    total = None
    for step in range(1, size):
        sent = block_of(step).astype(jnp.bfloat16)
        taken = shift_from(sent, axis, size, size - step).astype(jnp.float32)
        total = taken if total is None else total + taken
    own = block_of(0).astype(jnp.float32)
    return own if total is None else own + total


def swap_bit(array, axis, size, bit):
    return lax.ppermute(array, axis, [(i, i ^ (1 << bit)) for i in range(size)])


def halve(block, axis, size, bit):
    half = block.shape[0] // 2
    mine = (lax.axis_index(axis) >> bit) & 1
    sent = lax.dynamic_slice_in_dim(block, (1 - mine) * half, half, axis=0)
    kept = lax.dynamic_slice_in_dim(block, mine * half, half, axis=0)
    taken = swap_bit(sent, axis, size, bit)
    return (kept.astype(jnp.float32) + taken.astype(jnp.float32)).astype(jnp.bfloat16)


def double(block, axis, size, bit):
    mine = (lax.axis_index(axis) >> bit) & 1
    taken = swap_bit(block, axis, size, bit)
    first = jnp.where(mine == 0, block, taken)
    second = jnp.where(mine == 0, taken, block)
    return jnp.concatenate([first, second], axis=0)


def bit_orders(size):
    bits = list(range(size.bit_length() - 1))
    if len(bits) == 4:
        return ([0, 1, 2, 3], [1, 0, 3, 2], [2, 3, 0, 1])
    return tuple(bits[k:] + bits[:k] for k in range(3))


def sum_steps(size):
    orders = bit_orders(size)
    steps = [(halve, [order[k] for order in orders]) for k in range(len(orders[0]))]
    return steps + [(double, bits) for _, bits in reversed(steps)]


def thirds(stacked):
    return list(jnp.split(stacked, 3, axis=0))


def advance(blocks, axis, size, steps):
    for move, bits in steps:
        blocks = [move(block, axis, size, bit) for block, bit in zip(blocks, bits)]
    return blocks


def doubling_sum(array, axis, size):
    for bit in range(size.bit_length() - 1):
        array = array + swap_bit(array, axis, size, bit)
    return array


def on_device(
    reps,
    grps,
    inputs,
    clip_lengths,
    first_gain,
    first_shift,
    query_weight,
    query_bias,
    key_weight,
    value_weight,
    value_bias,
    output_weight,
    output_bias,
    second_gain,
    second_shift,
    up_weight,
    up_bias,
    down_weight,
    down_bias,
    out_grad,
):
    core = lax.axis_index("grp")
    vectors = (
        first_gain,
        first_shift,
        query_bias,
        value_bias,
        output_bias,
        second_gain,
        second_shift,
        down_bias,
        up_bias,
    )
    packed = lax.all_gather(jnp.concatenate(vectors), "grp", axis=0, tiled=False)
    unpacked, at = [], 0
    for vector in vectors:
        unpacked.append(packed[:, at : at + vector.shape[0]].reshape(-1))
        at += vector.shape[0]
    (
        gain_before,
        shift_before,
        query_offset,
        value_offset,
        output_offset,
        gain_middle,
        shift_middle,
        down_offset,
        up_offset,
    ) = unpacked
    key_matrix = gather_turned(key_weight, "grp", grps, 0)
    value_matrix = gather_turned(value_weight, "grp", grps, 0)
    query_matrix = gather_turned(query_weight, "grp", grps, 0)
    output_matrix = lax.all_gather(output_weight, "grp", axis=0, tiled=True)
    up_matrix = lax.all_gather(up_weight, "grp", axis=0, tiled=True)
    down_matrix = lax.all_gather(down_weight, "grp", axis=0, tiled=True)
    width = first_gain.shape[0]
    wide = up_bias.shape[0]
    frames = inputs.shape[1]

    normed_in, norm_one, inverse_one = layer_norm(inputs, gain_before, shift_before)
    turned = turn(normed_in, grps, 2, core)
    keys = matmul(turned, key_matrix).astype(jnp.bfloat16)
    values = (matmul(turned, value_matrix) + value_offset.astype(jnp.float32)).astype(
        jnp.bfloat16
    )
    all_keys = gather_turned(keys, "grp", grps, 1)
    all_values = gather_turned(values, "grp", grps, 1)
    query = (matmul(turned, query_matrix) + query_offset.astype(jnp.float32)).astype(
        jnp.bfloat16
    )
    slot = lax.iota(jnp.int32, grps * frames)
    position = lax.rem(slot + core * frames, grps * frames)
    valid = (position < clip_lengths[0]).astype(jnp.float32)[:, None]
    attended, logsum = attention_forward(query[0], all_keys[0], all_values[0], valid)
    attended = attended[None]
    middle = inputs + matmul(attended, output_matrix) + output_offset.astype(jnp.float32)
    normed_mid, norm_two, inverse_two = layer_norm(middle, gain_middle, shift_middle)
    pre = matmul(normed_mid, up_matrix) + up_offset.astype(jnp.float32)
    hidden = gelu_value(pre).astype(jnp.bfloat16)
    block_out = middle + matmul(hidden, down_matrix) + down_offset.astype(jnp.float32)

    def columns(array, step, extent):
        start = lax.rem(core + step, grps) * extent
        return lax.dynamic_slice_in_dim(array, start, extent, axis=2)

    grad_low = out_grad.astype(jnp.bfloat16)
    down_grad = scatter_sum(
        lambda step: outer_sum(columns(hidden, step, wide), grad_low), "grp", grps
    )
    down_offset_grad = jnp.sum(out_grad, axis=(0, 1))
    pre_grad = back_matmul(grad_low, down_matrix) * gelu_slope(pre)
    pre_low = pre_grad.astype(jnp.bfloat16)
    up_grad = scatter_sum(
        lambda step: outer_sum(columns(normed_mid, step, width), pre_low), "grp", grps
    )
    full = down_weight.shape[1]
    pieces = up_grad.shape[1] // full
    stacked = jnp.concatenate(
        [down_grad.astype(jnp.bfloat16)]
        + [up_grad[:, k * full : (k + 1) * full].astype(jnp.bfloat16) for k in range(pieces)],
        axis=0,
    )
    early = thirds(stacked)
    up_offset_grad = jnp.sum(pre_grad, axis=(0, 1))
    middle_part, gain_middle_grad, shift_middle_grad = norm_backward(
        back_matmul(pre_low, up_matrix), norm_two, inverse_two, gain_middle
    )
    middle_grad = out_grad + middle_part
    middle_low = middle_grad.astype(jnp.bfloat16)
    output_grad = scatter_sum(
        lambda step: outer_sum(columns(attended, step, width), middle_low), "grp", grps
    )
    output_offset_grad = jnp.sum(middle_grad, axis=(0, 1))
    attended_grad = back_matmul(middle_low, output_matrix).astype(jnp.bfloat16)
    steps = sum_steps(reps)
    bits = len(steps) // 2
    early, attended_grad = lax.optimization_barrier((early, attended_grad))
    stages = (steps[:1], steps[1:2], steps[2:bits])
    parts = []
    count = PAIRS // len(stages)
    for stage, moves in enumerate(stages):
        early = advance(early, "rep", reps, moves)
        part = attention_backward(
            query[0],
            all_keys[0],
            all_values[0],
            attended[0],
            attended_grad[0],
            logsum,
            valid,
            stage * count,
            count,
        )
        early, attended_grad, part = lax.optimization_barrier((early, attended_grad, part))
        parts.append(part)
    query_grad, key_part, value_part = (
        jnp.concatenate([part[k] for part in parts], axis=1)[None] for k in range(3)
    )
    early = advance(early, "rep", reps, steps[bits : 2 * bits - 2])
    value_grad = scatter_sum(
        lambda step: value_part[:, step * frames : (step + 1) * frames], "grp", grps
    )
    key_grad = scatter_sum(
        lambda step: key_part[:, step * frames : (step + 1) * frames], "grp", grps
    )
    query_grad, early = lax.optimization_barrier((query_grad, early))
    early = advance(early, "rep", reps, steps[2 * bits - 2 :])
    query_low = query_grad.astype(jnp.bfloat16)
    key_low = key_grad.astype(jnp.bfloat16)
    value_low = value_grad.astype(jnp.bfloat16)

    def turned_outer(low):
        return scatter_sum(
            lambda step: outer_sum(turned[:, :, step * width : (step + 1) * width], low),
            "grp",
            grps,
        )

    query_matrix_grad = turned_outer(query_low)
    value_matrix_grad = turned_outer(value_low)
    key_matrix_grad = turned_outer(key_low)
    late = jnp.concatenate(
        [
            grad.astype(jnp.bfloat16)
            for grad in (output_grad, query_matrix_grad, value_matrix_grad, key_matrix_grad)
        ],
        axis=0,
    )
    late = advance(thirds(late), "rep", reps, steps[:1])
    query_offset_grad = jnp.sum(query_grad, axis=(0, 1))
    value_offset_grad = jnp.sum(value_grad, axis=(0, 1))
    upstream_in = turn(
        back_matmul(query_low, query_matrix)
        + back_matmul(key_low, key_matrix)
        + back_matmul(value_low, value_matrix),
        grps,
        2,
        lax.rem(grps - core, grps),
    )
    input_part, gain_before_grad, shift_before_grad = norm_backward(
        upstream_in, norm_one, inverse_one, gain_before
    )
    input_grad = middle_grad + input_part

    summed = jnp.concatenate(
        [
            grad.reshape(grps, -1)
            for grad in (
                gain_before_grad,
                shift_before_grad,
                query_offset_grad,
                value_offset_grad,
                output_offset_grad,
                gain_middle_grad,
                shift_middle_grad,
                down_offset_grad,
                up_offset_grad,
            )
        ],
        axis=1,
    )
    summed = scatter_sum(
        lambda step: lax.dynamic_index_in_dim(
            summed, lax.rem(core + step, grps), 0, keepdims=False
        ).reshape(-1, 128),
        "grp",
        grps,
    )
    late, summed = lax.optimization_barrier((late, summed))
    late = jnp.concatenate(advance(late, "rep", reps, steps[1:]), axis=0)
    summed = doubling_sum(summed, "rep", reps).reshape(-1)

    def vector(k):
        return summed[k * width : (k + 1) * width]

    late = late.astype(jnp.float32)
    early = jnp.concatenate(early, axis=0).astype(jnp.float32)
    up_rows = early[wide:]
    return (
        block_out,
        input_grad,
        vector(0),
        vector(1),
        late[width : 2 * width],
        vector(2),
        late[3 * width :],
        late[2 * width : 3 * width],
        vector(3),
        late[:width],
        vector(4),
        vector(5),
        vector(6),
        jnp.concatenate([up_rows[k * width : (k + 1) * width] for k in range(pieces)], axis=1),
        summed[8 * width :],
        early[:wide],
        vector(7),
    )


def solution(mesh):
    return jax.shard_map(
        functools.partial(on_device, mesh.shape["rep"], mesh.shape["grp"]),
        mesh=mesh,
        in_specs=(
            P("rep", "grp", None),
            P("rep"),
            P("grp"),
            P("grp"),
            P("grp", None),
            P("grp"),
            P("grp", None),
            P("grp", None),
            P("grp"),
            P("grp", None),
            P("grp"),
            P("grp"),
            P("grp"),
            P("grp", None),
            P("grp"),
            P("grp", None),
            P("grp"),
            P("rep", "grp", None),
        ),
        out_specs=(
            P("rep", "grp", None),
            P("rep", "grp", None),
            P("grp"),
            P("grp"),
            P("grp", None),
            P("grp"),
            P("grp", None),
            P("grp", None),
            P("grp"),
            P("grp", None),
            P("grp"),
            P("grp"),
            P("grp"),
            P("grp", None),
            P("grp"),
            P("grp", None),
            P("grp"),
        ),
        check_vma=False,
    )
```
